32 devices in a mesh: grp: 2 (over x), fsdp: 4 (over z), tp: 4 (over y, core).
Axes of the slice: x: 2, y: 2, z: 4, core: 2. Of those that a mesh axis runs over, the one named last changes fastest.
Arguments:
- learn_hidden: bfloat16 [8192, 14336], P(('grp', 'fsdp'), 'tp'), may hold values from -6 to 6
- learn_cotangent: bfloat16 [8192, 4096], P(('grp', 'fsdp')), may hold values from -0.09375 to 0.09375
- master_weight: float32 [4096, 14336], P(('grp', 'fsdp'), 'tp'), may hold values from -0.046875 to 0.046875
- momentum: float32 [4096, 14336], P(('grp', 'fsdp'), 'tp'), may hold values from -6 to 6
- roll_hidden: bfloat16 [256, 14336], P(('grp', 'fsdp'), 'tp'), may hold values from -6 to 6
Outputs:
- momentum_new: float32 [4096, 14336], P(('grp', 'fsdp'), 'tp')
- roll_out: bfloat16 [256, 4096], P(('grp', 'fsdp'))
The draws below stay inside these ranges and needn't reach their ends.
All inputs are finite; a program needn't handle non-finite values.
Results may differ from the reference program's by a relative error of at most 0.015.
Values may be sent and summed in bfloat16 or wider, within the bound.
A program may use at most 128 MiB of HBM per device.

```python
import jax
import jax.numpy as jnp
from jax import lax

D = 4096
FF = 14336
TOK_DEV = 1024
TOKENS = 8192
ROLLS = 256
N_GRP = 2
N_FSDP = 4


def with_spikes(drawn, rng, source, target, shards_of, factor):
    owner, partner = [(jnp.arange(drawn.shape[position]) // (drawn.shape[position] // shards_of)).reshape([-1 if axis == position else 1 for axis in range(drawn.ndim)]) for position in (source, target)]
    chosen = jax.random.permutation(rng, shards_of)[partner]
    strong = (owner == chosen) | (owner == (partner + shards_of // 2) % shards_of)
    return jnp.where(strong, factor * drawn, drawn)


def steps_of(stream_key, extent, pieces, smallest, top_value):
    def one(dim, parts):
        draws = jax.random.uniform(jax.random.fold_in(jax.random.fold_in(stream_key, 6), dim), (parts,), jnp.float32, smallest / len(pieces), top_value / len(pieces))
        return jnp.repeat(jnp.exp(draws), extent[dim] // parts).reshape((-1,) + (1,) * (len(extent) - dim - 1))

    factor_of = one(*pieces[0])
    for cut in pieces[1:]:
        factor_of = factor_of * one(*cut)
    return factor_of


def bell_draw(key, shape, spread, limit, pieces=(), held_as=jnp.bfloat16):
    values = jax.random.normal(key, shape, jnp.float32) * spread
    if len(pieces) > 0:
        values = steps_of(key, shape, pieces, -0.22, 0.18) * values
    return jnp.clip(values, min=-limit, max=limit).astype(held_as)


def noise_with(stream_key, dims, deviation, most, split, heavy, held_as=jnp.bfloat16):
    entries = deviation * jax.random.normal(stream_key, dims, jnp.float32)
    if split:
        entries = entries * steps_of(stream_key, dims, split, -0.22, 0.18)
    return jnp.clip(with_spikes(entries, jax.random.fold_in(stream_key, 3), *heavy), -most, most).astype(held_as)


def setup_inputs(seed: int = 0) -> dict:
    streams_of = jax.random.split(jax.random.key(seed), 6)
    return {
        "learn_hidden": bell_draw(streams_of[0], (TOKENS, FF), 1.0, 6.0, ((0, 8), (1, 4))),
        "learn_cotangent": noise_with(streams_of[1], (TOKENS, D), (TOKENS ** -0.5), 0.09375, ((0, 8),), (0, 1, 8, 2.0)),
        "master_weight": bell_draw(streams_of[2], (D, FF), FF ** -0.5, 0.046875, ((0, 8), (1, 4)), jnp.float32),
        "momentum": bell_draw(streams_of[3], (D, FF), 1.0, 6.0, ((0, 8), (1, 4)), jnp.float32),
        "roll_hidden": bell_draw(streams_of[4], (ROLLS, FF), 1.0, 6.0, ((0, 8), (1, 4))),
    }


MOMENTUM = 0.9
LEARN_RATE = 0.002


def reference(learn_hidden, learn_cotangent, master_weight, momentum, roll_hidden):
    groups = N_GRP * N_FSDP
    cot_groups = learn_cotangent.reshape(groups, TOK_DEV, D)
    hid_groups = learn_hidden.reshape(groups, TOK_DEV, FF)

    def add_group(total, pair):
        cot, hid = pair
        term = lax.dot_general(cot, hid, (((0,), (0,)), ((), ())), preferred_element_type=jnp.float32)
        rounded = lax.optimization_barrier(term.astype(jnp.bfloat16))
        return total + rounded.astype(jnp.float32), None

    grad, _ = lax.scan(add_group, jnp.zeros((D, FF), jnp.float32), (cot_groups, hid_groups))
    momentum_new = MOMENTUM * momentum + grad
    rollout_weight = (master_weight - LEARN_RATE * momentum_new).astype(jnp.bfloat16)
    roll_out = lax.dot_general(roll_hidden, rollout_weight, (((1,), (1,)), ((), ())), preferred_element_type=jnp.float32).astype(jnp.bfloat16)
    return momentum_new, roll_out
```

```python
import functools

import jax
import jax.numpy as jnp
from jax import lax
from jax.experimental import pallas as pl
from jax.experimental.pallas import tpu as pltpu
from jax.sharding import PartitionSpec as P

MESH = pl.DeviceIdType.MESH
MOMENTUM = 0.9
LEARN_RATE = 0.002
TOKENS_FIRST = (((0,), (0,)), ((), ()))
LAG = 2


def remote(src, dst, send_sem, recv_sem, target):
    return pltpu.make_async_remote_copy(
        src_ref=src, dst_ref=dst, send_sem=send_sem, recv_sem=recv_sem, device_id=target, device_id_type=MESH
    )


def grad_kernel(
    n, n_tp, cot_hbm, hid_hbm, grad_hbm,
    cot, own, other, term, recv, total,
    cot_local, own_sem, cot_send, cot_recv, hid_send, hid_recv, send_sem, recv_sem, out_sem,
):
    g, f, t = lax.axis_index("grp"), lax.axis_index("fsdp"), lax.axis_index("tp")
    chunks, tokens, width = own.shape
    rows = total.shape[0]
    half = n * rows
    share = tokens // n_tp
    pairs = n_tp // 2
    y, core = t // 2, t % 2
    peer = {"grp": 1 - g}
    partner = y * 2 + (1 - core)

    def mate(step):
        return lax.rem(y + step, pairs) * 2 + core

    barrier = pltpu.get_barrier_semaphore()
    pl.semaphore_signal(barrier, inc=1, device_id=peer, device_id_type=MESH)
    pl.semaphore_signal(barrier, inc=1, device_id={"tp": partner}, device_id_type=MESH)
    for step in range(1, pairs):
        pl.semaphore_signal(barrier, inc=1, device_id={"tp": mate(step)}, device_id_type=MESH)

    @pl.when(f > 0)
    def _():
        pl.semaphore_signal(barrier, inc=1, device_id={"fsdp": f - 1}, device_id_type=MESH)

    @pl.when(f < n - 1)
    def _():
        pl.semaphore_signal(barrier, inc=1, device_id={"fsdp": f + 1}, device_id_type=MESH)

    peers = 1 + pairs + (f > 0).astype(jnp.int32) + (f < n - 1).astype(jnp.int32)
    pl.semaphore_wait(barrier, peers)

    def cot_block(b):
        return cot.at[pl.ds(pl.multiple_of(tokens + b * share, share), share), :]

    def hid_cols(k):
        return hid_hbm.at[:, pl.ds(pl.multiple_of(k * width, width), width)]

    first_cot = remote(
        cot_hbm.at[pl.ds(pl.multiple_of(t * share, share), share), pl.ds(pl.multiple_of((1 - g) * half, half), half)],
        cot_block(t), cot_send.at[0], cot_recv.at[t], peer,
    )
    first_cot.start()

    def hidden_copy(k):
        return remote(hid_cols(k), other.at[k], hid_send.at[k], hid_recv.at[k], peer)

    def own_copy(k):
        return pltpu.make_async_copy(hid_cols(k), own.at[k], own_sem.at[k])

    def start_hidden(k, _):
        hidden_copy(k).start()
        return 0

    lax.fori_loop(0, chunks, start_hidden, 0)
    own_cot = pltpu.make_async_copy(
        cot_hbm.at[:, pl.ds(pl.multiple_of(g * half, half), half)], cot.at[pl.ds(0, tokens), :], cot_local.at[0]
    )
    own_cot.start()

    def start_own(k, _):
        own_copy(k).start()
        return 0

    lax.fori_loop(0, chunks, start_own, 0)

    first_cot.wait_recv()
    sends = []
    for step in range(1, pairs):
        sends.append(remote(cot_block(t), cot_block(t), cot_send.at[step], cot_recv.at[t], {"tp": mate(step)}))
        sends[-1].start()
    sends.append(remote(cot_block(t), cot_block(t), cot_send.at[pairs], cot_recv.at[t], {"tp": partner}))
    sends[-1].start()
    for step in range(1, pairs):
        b = mate(step)
        arrived = remote(cot_block(b), cot_block(b), cot_send.at[pairs + step], cot_recv.at[b], {"tp": partner})
        arrived.wait_recv()
        arrived.start()
        sends.append(arrived)
    for step in range(pairs):
        b = lax.rem(y + step, pairs) * 2 + (1 - core)
        remote(cot_block(b), cot_block(b), cot_send.at[0], cot_recv.at[b], {"tp": partner}).wait_recv()
    own_cot.wait()

    def up_copy(k, c):
        return remote(term.at[k, c], recv.at[k, c + 1], send_sem.at[k, c], recv_sem.at[k, c + 1], {"fsdp": lax.rem(f + 1, n)})

    def down_copy(k, c):
        return remote(term.at[k, c], recv.at[k, c], send_sem.at[k, c], recv_sem.at[k, c], {"fsdp": lax.rem(f + n - 1, n)})

    def arrived(k, slot):
        remote(term.at[k, 0], recv.at[k, slot], send_sem.at[k, 0], recv_sem.at[k, slot], {"fsdp": lax.rem(f + 1, n)}).wait_recv()

    def compute(k):
        own_copy(k).wait()
        hidden_copy(k).wait_recv()

        def one(i, _):
            c = jnp.where(f == n - 1, i, n - 1 - i)
            cols = pl.ds(pl.multiple_of(c * rows, rows), rows)
            value = lax.dot_general(
                cot[pl.ds(0, tokens), cols], own[k], TOKENS_FIRST, preferred_element_type=jnp.float32
            ) + lax.dot_general(
                cot[pl.ds(tokens, tokens), cols], other[k], TOKENS_FIRST, preferred_element_type=jnp.float32
            )
            term[k, c] = value.astype(jnp.bfloat16)

            @pl.when((f == 0) & (c > 0))
            def _():
                up_copy(k, c).start()

            @pl.when((f == n - 1) & (c < n - 1))
            def _():
                down_copy(k, c).start()

            return 0

        lax.fori_loop(0, n, one, 0)

    def relay(k):
        def one(i, _):
            c = n - 1 - i

            @pl.when((f > 0) & (c > f))
            def _():
                arrived(k, c + 1)
                term[k, c] = term[k, c] + recv[k, c + 1]
                up_copy(k, c).start()

            @pl.when((f < n - 1) & (i < f))
            def _():
                arrived(k, i)
                term[k, i] = term[k, i] + recv[k, i]
                down_copy(k, i).start()

            return 0

        lax.fori_loop(0, n, one, 0)

    def out_copy(k):
        return pltpu.make_async_copy(
            total, grad_hbm.at[:, pl.ds(pl.multiple_of(k * width, width), width)], out_sem.at[0]
        )

    def finish(k):
        @pl.when(f > 0)
        def _():
            arrived(k, f + 1)

        @pl.when(f < n - 1)
        def _():
            arrived(k, f)

        @pl.when(k > 0)
        def _():
            out_copy(k).wait()

        total[...] = term[k, f].astype(jnp.float32)

        @pl.when(f > 0)
        def _():
            total[...] += recv[k, f + 1].astype(jnp.float32)

        @pl.when(f < n - 1)
        def _():
            total[...] += recv[k, f].astype(jnp.float32)

        out_copy(k).start()

    def step(it, _):
        @pl.when(it < chunks)
        def _():
            compute(it)

        @pl.when((it >= 1) & (it <= chunks))
        def _():
            relay(it - 1)

        @pl.when(it >= LAG)
        def _():
            finish(it - LAG)

        return 0

    lax.fori_loop(0, chunks + LAG, step, 0)
    out_copy(0).wait()
    first_cot.wait_send()
    for copy in sends:
        copy.wait_send()

    def drain(k, _):
        hidden_copy(k).wait_send()

        def one(c, _):
            @pl.when(c != f)
            def _():
                up_copy(k, c).wait_send()

            return 0

        return lax.fori_loop(0, n, one, 0)

    lax.fori_loop(0, chunks, drain, 0)


def local(n_grp, n_fsdp, n_tp, learn_hidden, learn_cotangent, master_weight, momentum, roll_hidden):
    tokens, features = learn_cotangent.shape
    units = learn_hidden.shape[1]
    rows = features // n_grp // n_fsdp
    width = 256
    chunks = units // width
    pairs = n_tp // 2
    roll_all = lax.all_gather(roll_hidden, ("grp", "fsdp"), axis=0, tiled=True)
    dma = pltpu.SemaphoreType.DMA
    grad = pl.pallas_call(
        functools.partial(grad_kernel, n_fsdp, n_tp),
        out_shape=jax.ShapeDtypeStruct((rows, units), jnp.float32),
        in_specs=[pl.BlockSpec(memory_space=pl.ANY)] * 2,
        out_specs=pl.BlockSpec(memory_space=pl.ANY),
        scratch_shapes=[
            pltpu.VMEM((n_grp * tokens, features // n_grp), jnp.bfloat16),
            pltpu.VMEM((chunks, tokens, width), jnp.bfloat16),
            pltpu.VMEM((chunks, tokens, width), jnp.bfloat16),
            pltpu.VMEM((chunks, n_fsdp, rows, width), jnp.bfloat16),
            pltpu.VMEM((chunks, n_fsdp + 1, rows, width), jnp.bfloat16),
            pltpu.VMEM((rows, width), jnp.float32),
            dma((1,)),
            dma((chunks,)),
            dma((2 * pairs,)),
            dma((n_tp,)),
            dma((chunks,)),
            dma((chunks,)),
            dma((chunks, n_fsdp)),
            dma((chunks, n_fsdp + 1)),
            dma((1,)),
        ],
        compiler_params=pltpu.CompilerParams(
            collective_id=0, has_side_effects=True, vmem_limit_bytes=60 * 1024 * 1024
        ),
        name="grad_rows",
    )(learn_cotangent, learn_hidden)
    momentum_new = MOMENTUM * momentum + grad
    rollout_weight = (master_weight - LEARN_RATE * momentum_new).astype(jnp.bfloat16)
    partial_out = lax.dot_general(
        roll_all, rollout_weight, (((1,), (1,)), ((), ())), preferred_element_type=jnp.float32
    ).astype(jnp.bfloat16)
    spread = lax.all_to_all(partial_out, ("grp", "fsdp"), split_axis=0, concat_axis=1, tiled=True)
    roll_out = lax.psum(spread, "tp")
    return (momentum_new, roll_out)


def solution(mesh):
    blocks = P(("grp", "fsdp"), "tp")
    whole_rows = P(("grp", "fsdp"), None)
    sizes = (mesh.shape["grp"], mesh.shape["fsdp"], mesh.shape["tp"])
    return jax.shard_map(
        functools.partial(local, *sizes),
        mesh=mesh,
        in_specs=(blocks, whole_rows, blocks, blocks, blocks),
        out_specs=(blocks, whole_rows),
        check_vma=False,
    )
```

```python
import functools

import jax
import jax.numpy as jnp
from jax import lax
from jax.experimental import pallas as pl
from jax.experimental.pallas import tpu as pltpu
from jax.sharding import PartitionSpec as P

MESH = pl.DeviceIdType.MESH
MOMENTUM = 0.9
LEARN_RATE = 0.002
TOKENS_FIRST = (((0,), (0,)), ((), ()))
END_LAG = 4
MID_LAG = 3


def remote(src, dst, send_sem, recv_sem, target):
    return pltpu.make_async_remote_copy(
        src_ref=src, dst_ref=dst, send_sem=send_sem, recv_sem=recv_sem, device_id=target, device_id_type=MESH
    )


def step_kernel(
    n, n_tp, cot_hbm, hid_hbm, weight_hbm, momentum_hbm, roll_hbm, new_hbm, out_ref,
    cot, own, other, term, recv, total, held, master, rolls, acc, parts, landed, reduced, final,
    cot_local, own_sem, cot_send, cot_recv, hid_send, hid_recv, send_sem, recv_sem, out_sem, in_sem,
    roll_send, roll_recv, tail_send, all_recv, sum_recv, gather_recv,
):
    g, f, t = lax.axis_index("grp"), lax.axis_index("fsdp"), lax.axis_index("tp")
    chunks, tokens, width = own.shape
    rows = total.shape[0]
    half = n * rows
    share = tokens // n_tp
    pairs = n_tp // 2
    y, core = t // 2, t % 2
    peer = {"grp": 1 - g}
    partner = y * 2 + (1 - core)

    def mate(step):
        return lax.rem(y + step, pairs) * 2 + core

    groups = 2 * n
    me = g * n + f
    batch = roll_hbm.shape[0]

    def place(index):
        return {"grp": index // n, "fsdp": lax.rem(index, n)}

    barrier = pltpu.get_barrier_semaphore()
    for step in range(1, groups):
        pl.semaphore_signal(barrier, inc=1, device_id=place(lax.rem(me + step, groups)), device_id_type=MESH)
    for step in range(1, n_tp):
        pl.semaphore_signal(barrier, inc=1, device_id={"tp": lax.rem(t + step, n_tp)}, device_id_type=MESH)
    pl.semaphore_wait(barrier, groups + n_tp - 2)

    def order(i):
        return jnp.where(f >= n // 2, i, n - 1 - i)

    def cot_block(c, b):
        return cot.at[
            pl.ds(pl.multiple_of(tokens + b * share, share), share), pl.ds(pl.multiple_of(c * rows, rows), rows)
        ]

    def hid_cols(k):
        return hid_hbm.at[:, pl.ds(pl.multiple_of(k * width, width), width)]

    def cot_copy(c):
        return remote(
            cot_hbm.at[
                pl.ds(pl.multiple_of(t * share, share), share),
                pl.ds(pl.multiple_of((1 - g) * half + c * rows, rows), rows),
            ],
            cot_block(c, t), cot_send.at[c, 0], cot_recv.at[c, t], peer,
        )

    def hidden_copy(k):
        return remote(hid_cols(k), other.at[k], hid_send.at[k], hid_recv.at[k], peer)

    def own_copy(k):
        return pltpu.make_async_copy(hid_cols(k), own.at[k], own_sem.at[k])

    def start_hidden(k, _):
        hidden_copy(k).start()
        return 0

    cot_copy(order(0)).start()
    hidden_copy(0).start()
    for i in range(1, n):
        cot_copy(order(i)).start()
    early = min(chunks, 6)
    lax.fori_loop(1, early, start_hidden, 0)
    own_cot = pltpu.make_async_copy(
        cot_hbm.at[:, pl.ds(pl.multiple_of(g * half, half), half)], cot.at[pl.ds(0, tokens), :], cot_local.at[0]
    )
    own_cot.start()

    def start_own(k, _):
        own_copy(k).start()
        return 0

    lax.fori_loop(0, chunks, start_own, 0)

    def roll_block(index):
        return rolls.at[pl.ds(pl.multiple_of(index * batch, batch), batch), :]

    own_roll = pltpu.make_async_copy(roll_hbm, roll_block(me), in_sem.at[2])
    own_roll.start()

    def roll_copy(step):
        return remote(
            roll_hbm, roll_block(me), roll_send.at[step], roll_recv.at[me], {"fsdp": lax.rem(f + step, n)}
        )

    for step in range(1, n):
        roll_copy(step).start()

    def cross_copy(step):
        index = g * n + lax.rem(f + step, n)
        return remote(roll_block(index), roll_block(index), roll_send.at[n + step], roll_recv.at[index], peer)

    def roll_arrived(index):
        remote(roll_block(index), roll_block(index), roll_send.at[0], roll_recv.at[index], peer).wait_recv()

    def mate_copy(c, step):
        return remote(cot_block(c, t), cot_block(c, t), cot_send.at[c, step], cot_recv.at[c, t], {"tp": mate(step)})

    def partner_copy(c, step):
        b = mate(step)
        return remote(
            cot_block(c, b), cot_block(c, b), cot_send.at[c, pairs + step], cot_recv.at[c, b], {"tp": partner}
        )

    def share_cot(c):
        cot_copy(c).wait_recv()
        for step in range(1, pairs):
            mate_copy(c, step).start()
        partner_copy(c, 0).start()
        for step in range(1, pairs):
            partner_copy(c, step).wait_recv()
            partner_copy(c, step).start()
        for step in range(pairs):
            b = lax.rem(y + step, pairs) * 2 + (1 - core)
            remote(cot_block(c, b), cot_block(c, b), cot_send.at[c, 0], cot_recv.at[c, b], {"tp": partner}).wait_recv()

    def up_copy(k, c):
        return remote(term.at[k, c], recv.at[k, c + 1], send_sem.at[k, c], recv_sem.at[k, c + 1], {"fsdp": lax.rem(f + 1, n)})

    def down_copy(k, c):
        return remote(term.at[k, c], recv.at[k, c], send_sem.at[k, c], recv_sem.at[k, c], {"fsdp": lax.rem(f + n - 1, n)})

    def arrived(k, slot):
        remote(term.at[k, 0], recv.at[k, slot], send_sem.at[k, 0], recv_sem.at[k, slot], {"fsdp": lax.rem(f + 1, n)}).wait_recv()

    def compute(k, opening):
        own_copy(k).wait()
        if not opening:
            hidden_copy(k).wait_recv()

        def one(i, _):
            c = order(i)
            if opening:
                share_cot(c)

                @pl.when(i == 0)
                def _():
                    hidden_copy(k).wait_recv()

            cols = pl.ds(pl.multiple_of(c * rows, rows), rows)
            value = lax.dot_general(
                cot[pl.ds(0, tokens), cols], own[k], TOKENS_FIRST, preferred_element_type=jnp.float32
            ) + lax.dot_general(
                cot[pl.ds(tokens, tokens), cols], other[k], TOKENS_FIRST, preferred_element_type=jnp.float32
            )
            term[k, c] = value.astype(jnp.bfloat16)

            @pl.when((f == 0) & (c > 0))
            def _():
                up_copy(k, c).start()

            @pl.when((f == n - 1) & (c < n - 1))
            def _():
                down_copy(k, c).start()

            return 0

        lax.fori_loop(0, n, one, 0)

    def relay(k):
        def one(i, _):
            c = n - 1 - i

            @pl.when((f > 0) & (c > f))
            def _():
                arrived(k, c + 1)
                term[k, c] = term[k, c] + recv[k, c + 1]
                up_copy(k, c).start()

            @pl.when((f < n - 1) & (i < f))
            def _():
                arrived(k, i)
                term[k, i] = term[k, i] + recv[k, i]
                down_copy(k, i).start()

            return 0

        lax.fori_loop(0, n, one, 0)

    def out_copy(k):
        return pltpu.make_async_copy(
            total, new_hbm.at[:, pl.ds(pl.multiple_of(k * width, width), width)], out_sem.at[0]
        )

    def in_copies(k):
        cols = pl.ds(pl.multiple_of(k * width, width), width)
        return (
            pltpu.make_async_copy(momentum_hbm.at[:, cols], held, in_sem.at[0]),
            pltpu.make_async_copy(weight_hbm.at[:, cols], master, in_sem.at[1]),
        )

    def finish(k):
        @pl.when(f > 0)
        def _():
            arrived(k, f + 1)

        @pl.when(f < n - 1)
        def _():
            arrived(k, f)

        @pl.when(k > 0)
        def _():
            out_copy(k).wait()

        total[...] = term[k, f].astype(jnp.float32)

        @pl.when(f > 0)
        def _():
            total[...] += recv[k, f + 1].astype(jnp.float32)

        @pl.when(f < n - 1)
        def _():
            total[...] += recv[k, f].astype(jnp.float32)

        for copy in in_copies(k):
            copy.wait()
        total[...] += MOMENTUM * held[...]
        out_copy(k).start()
        weight = (master[...] - LEARN_RATE * total[...]).astype(jnp.bfloat16)
        acc[...] += lax.dot_general(
            rolls[:, pl.ds(pl.multiple_of(k * width, width), width)],
            weight, (((1,), (1,)), ((), ())), preferred_element_type=jnp.float32,
        )

    own_cot.wait()
    compute(0, True)
    own_roll.wait()
    for step in range(1, n):
        roll_arrived(g * n + lax.rem(f + step, n))
    for step in range(n):
        cross_copy(step).start()
    lax.fori_loop(early, chunks, start_hidden, 0)
    acc[...] = jnp.zeros_like(acc)

    lag = jnp.where((f == 0) | (f == n - 1), END_LAG, MID_LAG)

    def iteration(it, _):
        @pl.when((it >= lag) & (it < chunks + lag))
        def _():
            for copy in in_copies(it - lag):
                copy.start()

        @pl.when(it < chunks)
        def _():
            compute(it, False)

        @pl.when((it >= 1) & (it <= chunks))
        def _():
            relay(it - 1)

        @pl.when(it == lag)
        def _():
            for step in range(n):
                roll_arrived((1 - g) * n + lax.rem(f + step, n))

        @pl.when((it >= lag) & (it < chunks + lag))
        def _():
            finish(it - lag)

        return 0

    lax.fori_loop(1, chunks + END_LAG, iteration, 0)

    tails = []
    for d in range(groups):
        parts[d] = acc[d * batch:(d + 1) * batch, :].astype(jnp.bfloat16)
    for step in range(1, groups):
        d = lax.rem(me + step, groups)
        tails.append(remote(parts.at[d], landed.at[me], tail_send.at[len(tails)], all_recv.at[me], place(d)))
        tails[-1].start()
    landed[me] = parts[me]
    for step in range(1, groups):
        d = lax.rem(me + step, groups)
        remote(parts.at[d], landed.at[d], tail_send.at[0], all_recv.at[d], place(d)).wait_recv()
    per = groups // n_tp
    mine = pl.ds(t * per, per)
    for step in range(1, n_tp):
        b = lax.rem(t + step, n_tp)
        tails.append(
            remote(landed.at[pl.ds(b * per, per)], reduced.at[t], tail_send.at[len(tails)], sum_recv.at[t], {"tp": b})
        )
        tails[-1].start()
    value = landed[mine].astype(jnp.float32)
    for step in range(1, n_tp):
        b = lax.rem(t + step, n_tp)
        remote(landed.at[mine], reduced.at[b], tail_send.at[0], sum_recv.at[b], {"tp": b}).wait_recv()
        value = value + reduced[b].astype(jnp.float32)
    final[mine] = value.astype(jnp.bfloat16)
    for step in range(1, n_tp):
        b = lax.rem(t + step, n_tp)
        tails.append(remote(final.at[mine], final.at[mine], tail_send.at[len(tails)], gather_recv.at[t], {"tp": b}))
        tails[-1].start()
    for step in range(1, n_tp):
        b = lax.rem(t + step, n_tp)
        theirs = pl.ds(b * per, per)
        remote(final.at[theirs], final.at[theirs], tail_send.at[0], gather_recv.at[b], {"tp": b}).wait_recv()
    for d in range(groups):
        out_ref[:, d * rows:(d + 1) * rows] = final[d]

    out_copy(0).wait()
    for copy in tails:
        copy.wait_send()
    for step in range(1, n):
        roll_copy(step).wait_send()
    for step in range(n):
        cross_copy(step).wait_send()

    def drain_cot(c, _):
        cot_copy(c).wait_send()
        for step in range(1, pairs):
            mate_copy(c, step).wait_send()
        for step in range(pairs):
            partner_copy(c, step).wait_send()
        return 0

    lax.fori_loop(0, n, drain_cot, 0)

    def drain(k, _):
        hidden_copy(k).wait_send()

        def one(c, _):
            @pl.when(c != f)
            def _():
                up_copy(k, c).wait_send()

            return 0

        return lax.fori_loop(0, n, one, 0)

    lax.fori_loop(0, chunks, drain, 0)


def local(n_grp, n_fsdp, n_tp, learn_hidden, learn_cotangent, master_weight, momentum, roll_hidden):
    tokens, features = learn_cotangent.shape
    units = learn_hidden.shape[1]
    rows = features // n_grp // n_fsdp
    width = 256
    chunks = units // width
    pairs = n_tp // 2
    groups = n_grp * n_fsdp
    batch = roll_hidden.shape[0]
    dma = pltpu.SemaphoreType.DMA
    small, wide = jnp.bfloat16, jnp.float32
    return tuple(pl.pallas_call(
        functools.partial(step_kernel, n_fsdp, n_tp),
        out_shape=(
            jax.ShapeDtypeStruct((rows, units), wide),
            jax.ShapeDtypeStruct((batch, features), small),
        ),
        in_specs=[pl.BlockSpec(memory_space=pl.ANY)] * 5,
        out_specs=(pl.BlockSpec(memory_space=pl.ANY), pl.BlockSpec(memory_space=pltpu.VMEM)),
        scratch_shapes=[
            pltpu.VMEM((n_grp * tokens, features // n_grp), small),
            pltpu.VMEM((chunks, tokens, width), small),
            pltpu.VMEM((chunks, tokens, width), small),
            pltpu.VMEM((chunks, n_fsdp, rows, width), small),
            pltpu.VMEM((chunks, n_fsdp + 1, rows, width), small),
            pltpu.VMEM((rows, width), wide),
            pltpu.VMEM((rows, width), wide),
            pltpu.VMEM((rows, width), wide),
            pltpu.VMEM((groups * batch, units), small),
            pltpu.VMEM((groups * batch, rows), wide),
            pltpu.VMEM((groups, batch, rows), small),
            pltpu.VMEM((groups, batch, rows), small),
            pltpu.VMEM((n_tp, groups // n_tp, batch, rows), small),
            pltpu.VMEM((groups, batch, rows), small),
            dma((1,)),
            dma((chunks,)),
            dma((n_fsdp, 2 * pairs)),
            dma((n_fsdp, n_tp)),
            dma((chunks,)),
            dma((chunks,)),
            dma((chunks, n_fsdp)),
            dma((chunks, n_fsdp + 1)),
            dma((1,)),
            dma((3,)),
            dma((2 * n_fsdp,)),
            dma((groups,)),
            dma((groups + 2 * n_tp,)),
            dma((groups,)),
            dma((n_tp,)),
            dma((n_tp,)),
        ],
        compiler_params=pltpu.CompilerParams(
            collective_id=0, has_side_effects=True, vmem_limit_bytes=60 * 1024 * 1024
        ),
        name="learner_step",
    )(learn_cotangent, learn_hidden, master_weight, momentum, roll_hidden))


def solution(mesh):
    blocks = P(("grp", "fsdp"), "tp")
    whole_rows = P(("grp", "fsdp"), None)
    sizes = (mesh.shape["grp"], mesh.shape["fsdp"], mesh.shape["tp"])
    return jax.shard_map(
        functools.partial(local, *sizes),
        mesh=mesh,
        in_specs=(blocks, whole_rows, blocks, blocks, blocks),
        out_specs=(blocks, whole_rows),
        check_vma=False,
    )
```
